32 devices in a mesh: ga: 8 (over y, x, core), band: 4 (over z).
Axes of the slice: x: 2, y: 2, z: 4, core: 2. Of those that a mesh axis runs over, the one named last changes fastest.
Arguments:
- waves: bfloat16 [2, 8192, 4096], P(None, 'ga', 'band'), may hold values from -6 to 6
- rotation: bfloat16 [2, 4096, 4096], P(None, 'ga', 'band'), may hold values from -0.0625 to 0.0625
Outputs:
- rotated: bfloat16 [2, 8192, 4096], P(None, 'ga', 'band')
The draws below stay inside these ranges and needn't reach their ends.
All inputs are finite; a program needn't handle non-finite values.
Results may differ from the reference program's by a relative error of at most 0.001.
Values may be sent and summed in bfloat16 or wider, within the bound.
No kernel may reach another device: no remote copies, remote signals or barrier semaphores. Data moves between devices by JAX's collectives and lax.ppermute only.
A program may use at most 128 MiB of HBM per device.

```python
import jax
import jax.numpy as jnp

NB = 4096
NG = 8192


def levels(rng, shape, split, least, high):
    level, own = 1.0, jax.random.fold_in(rng, 6)
    for position, blocks in split:
        heights = jnp.exp(jax.random.uniform(jax.random.fold_in(own, position), (blocks,), jnp.float32, least / len(split), high / len(split)))
        level = level * jnp.repeat(heights, shape[position] // blocks).reshape([-1 if axis == position else 1 for axis in range(len(shape))])
    return level


def normal_values(stream_key, extent, width, reach, cuts=(), kind=jnp.bfloat16):
    drawn = jax.random.normal(stream_key, extent, jnp.float32) * width
    if len(cuts) > 0:
        drawn = levels(stream_key, extent, cuts, -0.22, 0.18) * drawn
    return jnp.clip(drawn, min=-reach, max=reach).astype(kind)


def setup_inputs(seed: int = 0) -> dict:
    arg_keys = jax.random.split(jax.random.key(seed), 3)
    waves = normal_values(arg_keys[0], (2, NG, NB), 1.0, 6.0, ((1, 8), (2, 4)))
    rotation = normal_values(arg_keys[1], (2, NB, NB), (2 * NB) ** -0.5, 0.0625, ((1, 8), (2, 4)))
    return dict(waves=waves, rotation=rotation)


def reference(waves, rotation):
    stacked = jnp.concatenate([waves[0], waves[1]], axis=1)
    real_rows = jnp.concatenate([rotation[0], rotation[1]], axis=1)
    imag_rows = jnp.concatenate([-rotation[1], rotation[0]], axis=1)
    matrix = jnp.concatenate([real_rows, imag_rows], axis=0)
    result = jnp.dot(stacked, matrix, preferred_element_type=jnp.float32)
    return jnp.stack([result[:, :NB], result[:, NB:]]).astype(jnp.bfloat16)
```

```python
import functools

import jax
import jax.numpy as jnp
from jax import lax
from jax.experimental import pallas as pl
from jax.experimental.pallas import tpu as pltpu
from jax.sharding import PartitionSpec as P


INWARD = [(0, 1), (3, 2)]
OUTWARD = [(1, 0), (2, 3)]
MIDDLE = [(1, 2), (2, 1)]


def gathered(waves, rotation):
    cols_here = waves.shape[2]
    columns = lax.all_gather(rotation, "ga", axis=1, tiled=True)
    real_rows = jnp.concatenate([columns[0], columns[1]], axis=1)
    imag_rows = jnp.concatenate([-columns[1], columns[0]], axis=1)
    piece = lax.all_gather(waves, "band", axis=2, tiled=True)
    total = jnp.dot(piece[0], real_rows, preferred_element_type=jnp.float32)
    result = total + jnp.dot(piece[1], imag_rows, preferred_element_type=jnp.float32)
    return jnp.stack([result[:, :cols_here], result[:, cols_here:]]).astype(jnp.bfloat16)


def band(x, pairs, name):
    with jax.named_scope(name):
        return lax.ppermute(x, "band", pairs)


def swap(x, bit, size, name):
    with jax.named_scope(name):
        return lax.ppermute(x, "ga", [(i, i ^ bit) for i in range(size)])


def exchange(block, size, name):
    over_x = swap(block, 2, size, name + "_x")
    over_y = swap(block, 4, size, name + "_y")
    far_c = swap(over_y[0:1], 2, size, name + "_xy")
    far_d = swap(over_x[1:2], 4, size, name + "_yx")
    mine = jnp.stack([block, over_x, over_y, jnp.concatenate([far_c, far_d], axis=0)])
    return mine, swap(mine, 1, size, name + "_core")


def product_kernel(ways, table, *refs):
    slots, rest = refs[: sum(ways)], refs[sum(ways):]
    mine, other, out, left, total = rest
    step = pl.program_id(0)
    rows, half = out.shape[1], mine.shape[2]
    end, core = table[4], table[5]

    def fill(ref):
        for place, part in ((0, core), (1, 1 - core)):
            cols = pl.ds(pl.multiple_of(part * half, half), half)
            a, b = ref[0, :, cols], ref[1, :, cols]
            base = place * 2 * half
            left[:rows, base : base + half] = a
            left[:rows, base + half : base + 2 * half] = -b
            left[rows:, base : base + half] = b
            left[rows:, base + half : base + 2 * half] = a

    at = 0
    for slot, count in enumerate(ways):
        if count == 1:
            pl.when(step == slot)(functools.partial(fill, slots[at]))
        else:
            pl.when((step == slot) & (end == 0))(functools.partial(fill, slots[at]))
            pl.when((step == slot) & (end == 1))(functools.partial(fill, slots[at + 1]))
        at += count

    @pl.when(step == 0)
    def _():
        total[...] = jnp.zeros_like(total)

    width = min(256, out.shape[2])

    @pl.loop(0, out.shape[2] // width)
    def _(n):
        cols = pl.ds(pl.multiple_of(n * width, width), width)
        first = mine[0, :, :, cols].reshape(2 * half, width)
        second = other[0, :, :, cols].reshape(2 * half, width)
        total[:, cols] += jnp.dot(left[:, : 2 * half], first, preferred_element_type=jnp.float32) + jnp.dot(
            left[:, 2 * half :], second, preferred_element_type=jnp.float32
        )

    @pl.when(step == pl.num_programs(0) - 1)
    def _():
        out[0] = total[:rows].astype(out.dtype)
        out[1] = total[rows:].astype(out.dtype)


def product(table, slots, matrix, rows, name):
    mine, other = matrix
    half, cols = mine.shape[2], mine.shape[3]
    depth = 2 * half
    flat = [piece for slot in slots for piece in slot]

    def rows_at(first):
        assert first % rows == 0
        return lambda step, table: (0, first // rows, 0)

    specs = [pl.BlockSpec((2, rows, depth), rows_at(first), pipeline_mode=pl.Buffered(1)) for _, first in flat]
    block = pl.BlockSpec((1, 2, half, cols), lambda step, table: (table[step], 0, 0, 0))
    with jax.named_scope(name):
        return pl.pallas_call(
            functools.partial(product_kernel, tuple(len(slot) for slot in slots)),
            out_shape=jax.ShapeDtypeStruct((2, rows, cols), jnp.bfloat16),
            grid_spec=pltpu.PrefetchScalarGridSpec(
                num_scalar_prefetch=1,
                grid=(len(slots),),
                in_specs=specs + [block, block],
                out_specs=pl.BlockSpec((2, rows, cols), lambda step, table: (0, 0, 0)),
                scratch_shapes=[pltpu.VMEM((2 * rows, 2 * depth), jnp.bfloat16), pltpu.VMEM((2 * rows, cols), jnp.float32)],
            ),
            compiler_params=pltpu.CompilerParams(dimension_semantics=("arbitrary",), vmem_limit_bytes=40 << 20),
            cost_estimate=pl.CostEstimate(
                flops=2 * 4 * rows * depth * len(slots) * cols,
                bytes_accessed=2 * 2 * len(slots) * depth * cols + 2 * 2 * rows * (depth * len(flat) + cols),
                transcendentals=0,
            ),
            name=name,
        )(table, *[array for array, _ in flat], mine, other)


def hybrid(planes, waves, rotation):
    rows = waves.shape[1]
    quarter = rows // 4
    z, g = lax.axis_index("band"), lax.axis_index("ga")
    end = ((z == 0) | (z == 3)).astype(jnp.int32)
    chip = g // 2
    near, far = z ^ (3 - end), z ^ (2 + end)
    table = jnp.stack([z ^ chip, (z ^ 1) ^ chip, near ^ chip, far ^ chip, end, g % 2]).astype(jnp.int32)

    a_rows = 2 * quarter
    pieces_a = [(0, quarter), (quarter, quarter)]
    pieces_b = [(a_rows, quarter), (a_rows + quarter, quarter // 2), (a_rows + quarter + quarter // 2, quarter // 2)]

    def part(first, count):
        return lax.slice_in_dim(waves, first, first + count, axis=1)

    own_a, own_b = part(0, a_rows), part(a_rows, rows - a_rows)

    outer = band(rotation, INWARD, "in_r")
    mid_a = band(own_a, MIDDLE, "mid_a")
    out_1 = band(own_a, OUTWARD, "out_1")
    in_a = [band(part(*p), INWARD, f"in_a{i}") for i, p in enumerate(pieces_a)]
    in_b = [band(part(*p), INWARD, f"in_b{i}") for i, p in enumerate(pieces_b)]
    mid_b = band(own_b, MIDDLE, "mid_b")
    out_2 = band(mid_a, OUTWARD, "out_2")
    far_a = [band(x, MIDDLE, f"far_a{i}") for i, x in enumerate(in_a)]
    out_3 = [band(x, OUTWARD, f"out_3{i}") for i, x in enumerate(far_a)]
    far_b = [band(x, MIDDLE, f"far_b{i}") for i, x in enumerate(in_b)]

    matrix = exchange(rotation, planes, "own")
    matrix_outer = exchange(outer, planes, "outer")

    done = []
    for i, (first, count) in enumerate(pieces_a):
        slots = [
            [(waves, first)],
            [(in_a[i], 0), (out_1, first)],
            [(mid_a, first), (out_2, first)],
            [(far_a[i], 0), (out_3[i], 0)],
        ]
        done.append(product(table, slots, matrix, count, f"own_a{i}"))
    for i, (first, count) in enumerate(pieces_b):
        slots = [[(waves, first)], [(in_b[i], 0)], [(mid_b, first - a_rows)], [(far_b[i], 0)]]
        for_end = product(table, slots, matrix_outer, count, f"outer_b{i}")
        result = band(for_end, OUTWARD, f"result_{i}")
        here = product(table, slots, matrix, count, f"own_b{i}")
        done.append(jnp.where(end == 1, result, here))
    return jnp.concatenate(done, axis=1)


def solution(mesh):
    planes, line = mesh.shape["ga"], mesh.shape["band"]
    body = functools.partial(hybrid, planes) if (planes, line) == (8, 4) else gathered
    return jax.shard_map(
        body,
        mesh=mesh,
        in_specs=(P(None, "ga", "band"), P(None, "ga", "band")),
        out_specs=P(None, "ga", "band"),
        check_vma=False,
    )
```
